32 devices in a mesh: dp: 4 (over y, x), row: 4 (over z), col: 2 (over core).
Axes of the slice: x: 2, y: 2, z: 4, core: 2. Of those that a mesh axis runs over, the one named last changes fastest.
Arguments:
- image: bfloat16 [4, 256, 96, 256], P('dp', None, 'row', 'col'), may hold values from -6 to 6
- cotangent: bfloat16 [4, 256, 96, 256], P('dp', None, 'row', 'col'), may hold values from -6 to 6
- w_reduce: bfloat16 [256, 64], replicated, may hold values from -0.375 to 0.375
- w_spatial: bfloat16 [3, 3, 64, 64], replicated, may hold values from -0.25 to 0.25
- w_expand: bfloat16 [64, 256], replicated, may hold values from -0.75 to 0.75
Outputs:
- grad_image: bfloat16 [4, 256, 96, 256], P('dp', None, 'row', 'col')
- grad_reduce: float32 [256, 64], replicated
- grad_spatial: float32 [3, 3, 64, 64], replicated
- grad_expand: float32 [64, 256], replicated
The draws below stay inside these ranges and needn't reach their ends.
All inputs are finite; a program needn't handle non-finite values.
Results may differ from the reference program's by a relative error of at most 0.0061.
Values may be sent and summed in bfloat16 or wider, within the bound.
A program may use at most 64 MiB of HBM per device.

```python
import jax
import jax.numpy as jnp
from jax import lax

C = 256
M = 64
SLIDES = 4
NH = 96
NW = 256
PIXELS = 98304


def block_scale(own_key, extent, pieces, low, largest):
    def one(position, blocks):
        draws = jax.random.uniform(jax.random.fold_in(jax.random.fold_in(own_key, 6), position), (blocks,), jnp.float32, low / len(pieces), largest / len(pieces))
        return jnp.repeat(jnp.exp(draws), extent[position] // blocks).reshape((-1,) + (1,) * (len(extent) - position - 1))

    gain = one(*pieces[0])
    for cut in pieces[1:]:
        gain = gain * one(*cut)
    return gain


def normal_values(own_key, shape, spread, most, shards=(), kind=jnp.bfloat16):
    values = spread * jax.random.normal(own_key, shape, jnp.float32)
    if shards:
        values = values * block_scale(own_key, shape, shards, -0.22, 0.18)
    return jnp.clip(values, -most, most).astype(kind)


def setup_inputs(seed: int = 0) -> dict:
    key_of = jax.random.split(jax.random.key(seed), 6)
    image = normal_values(key_of[0], (SLIDES, C, NH, NW), 1.0, 6.0, ((0, 4), (2, 4), (3, 2)))
    cotangent = normal_values(key_of[1], (SLIDES, C, NH, NW), 1.0, 6.0, ((0, 4), (2, 4), (3, 2)))
    w_reduce = normal_values(key_of[2], (C, M), C ** -0.5, 0.375)
    w_spatial = normal_values(key_of[3], (3, 3, M, M), (9 * M) ** -0.5, 0.25)
    w_expand = normal_values(key_of[4], (M, C), M ** -0.5, 0.75)
    return {"image": image, "cotangent": cotangent, "w_reduce": w_reduce, "w_spatial": w_spatial, "w_expand": w_expand}


GELU_C = 0.7978845608028654
GELU_K = 0.044715


def gelu(v):
    t = jnp.tanh(GELU_C * (v + GELU_K * v * v * v))
    return 0.5 * v * (1.0 + t)


def slope(v):
    t = jnp.tanh(GELU_C * (v + GELU_K * v * v * v))
    return 0.5 * (1.0 + t) + 0.5 * v * (1.0 - t * t) * GELU_C * (1.0 + 3.0 * GELU_K * v * v)


def round_trip(v):
    return lax.optimization_barrier(v.astype(jnp.bfloat16)).astype(jnp.float32)


def reference(image, cotangent, w_reduce, w_spatial, w_expand):
    reduce_f = w_reduce.astype(jnp.float32)
    spatial_f = w_spatial.astype(jnp.float32)
    expand_f = w_expand.astype(jnp.float32)

    def one_slide(carry, pair):
        feats = pair[0].astype(jnp.float32)
        upstream = pair[1].astype(jnp.float32)
        height = feats.shape[1]
        width = feats.shape[2]
        pre_one = jnp.einsum('chw,cm->mhw', feats, reduce_f)
        hidden_one = round_trip(gelu(pre_one))
        pad_one = jnp.pad(hidden_one, ((0, 0), (1, 1), (1, 1)))
        pre_two = jnp.zeros((M, height, width), jnp.float32)
        for row_k in range(3):
            for col_k in range(3):
                window = pad_one[:, row_k:row_k + height, col_k:col_k + width]
                pre_two = pre_two + jnp.einsum('chw,cd->dhw', window, spatial_f[row_k, col_k])
        hidden_two = round_trip(gelu(pre_two))
        total = jnp.einsum('mhw,mc->chw', hidden_two, expand_f) + feats
        top = round_trip(upstream * slope(total))
        grad_expand = jnp.einsum('mhw,chw->mc', hidden_two, top)
        back_two = round_trip(jnp.einsum('chw,mc->mhw', top, expand_f) * slope(pre_two))
        pad_back = jnp.pad(back_two, ((0, 0), (1, 1), (1, 1)))
        tap_grads = []
        back_pre = jnp.zeros((M, height, width), jnp.float32)
        for row_k in range(3):
            for col_k in range(3):
                window = pad_one[:, row_k:row_k + height, col_k:col_k + width]
                tap_grads.append(jnp.einsum('chw,dhw->cd', window, back_two))
                moved = pad_back[:, 2 - row_k:2 - row_k + height, 2 - col_k:2 - col_k + width]
                back_pre = back_pre + jnp.einsum('dhw,cd->chw', moved, spatial_f[row_k, col_k])
        grad_spatial = jnp.stack(tap_grads).reshape(3, 3, M, M)
        back_one = round_trip(back_pre * slope(pre_one))
        grad_reduce = jnp.einsum('chw,mhw->cm', feats, back_one)
        result = (jnp.einsum('mhw,cm->chw', back_one, reduce_f) + top).astype(jnp.bfloat16)
        carry = (carry[0] + grad_reduce, carry[1] + grad_spatial, carry[2] + grad_expand)
        return carry, result

    start = (jnp.zeros((C, M), jnp.float32), jnp.zeros((3, 3, M, M), jnp.float32), jnp.zeros((M, C), jnp.float32))
    sums, grad_image = lax.scan(one_slide, start, (image, cotangent))
    scale = float(PIXELS) ** -0.5
    return grad_image, sums[0] * scale, sums[1] * scale, sums[2] * scale
```

```python
import functools

import jax
import jax.numpy as jnp
from jax import lax
from jax.experimental import pallas as pl
from jax.experimental.pallas import tpu as pltpu
from jax.sharding import PartitionSpec as P

GELU_C = 0.7978845608028654
GELU_K = 0.044715
F32 = jnp.float32
BF16 = jnp.bfloat16
AROUND = ((-1, 0), (1, 0), (-1, -1), (0, -1), (1, -1), (-1, 1), (0, 1), (1, 1))
R = 2


def gelu_slope(v):
    v2 = v * v
    t = jnp.tanh(GELU_C * (v + GELU_K * v2 * v))
    half = 0.5 * (1.0 + t)
    return v * half, half + 0.5 * v * (1.0 - t * t) * (GELU_C * (1.0 + 3.0 * GELU_K * v2))


def slope(v):
    return gelu_slope(v)[1]


def dot(a, b):
    return lax.dot_general(a, b, (((1,), (0,)), ((), ())), preferred_element_type=F32)


def dot_nt(a, b):
    return lax.dot_general(a, b, (((1,), (1,)), ((), ())), preferred_element_type=F32)


def kernel(sizes, image, cot, wr, wrt, w2, w3, we, wet, out, g_reduce, g_spatial, g_expand,
           xin, cin, xf, cf, xb, tb, s1, hid, back, edge, rows_in, cols_in,
           in_sem, send_sem, recv_sem):
    nrow, ncol = sizes
    channels, height, width = image.shape
    inner = we.shape[0]
    row, col = lax.axis_index("row"), lax.axis_index("col")
    lane = lax.broadcasted_iota(jnp.int32, (inner, width), 1)

    copy_x = pltpu.make_async_copy(image, xin, in_sem.at[0])
    copy_c = pltpu.make_async_copy(cot, cin, in_sem.at[1])
    copy_x.start()
    copy_c.start()

    def exists(dr, dc):
        ok = jnp.bool_(True)
        if dr:
            ok = jnp.logical_and(ok, (row > 0) if dr < 0 else (row < nrow - 1))
        if dc:
            ok = jnp.logical_and(ok, (col > 0) if dc < 0 else (col < ncol - 1))
        return ok

    barrier = pltpu.get_barrier_semaphore()
    for dr, dc in AROUND:
        @pl.when(exists(dr, dc))
        def _(dr=dr, dc=dc):
            pl.semaphore_signal(barrier, inc=1, device_id={"row": row + dr, "col": col + dc},
                                device_id_type=pl.DeviceIdType.MESH)
    pl.semaphore_wait(barrier, sum(exists(dr, dc).astype(jnp.int32) for dr, dc in AROUND))

    def halo_copy(turn, k, source):
        dr, dc = AROUND[k]
        if dc == 0:
            src = source.at[1 if dr < 0 else height, pl.ds(inner, inner)]
            dst = rows_in.at[turn, 1 if dr < 0 else 0]
        else:
            src = edge.at[turn, 0 if dc < 0 else 1]
            dst = cols_in.at[turn, 1 if dc < 0 else 0, 1 - dr]
        return pltpu.make_async_remote_copy(
            src_ref=src, dst_ref=dst, send_sem=send_sem.at[turn, k], recv_sem=recv_sem.at[turn, k],
            device_id={"row": row + dr, "col": col + dc}, device_id_type=pl.DeviceIdType.MESH)

    def halo_start(turn, source):
        for k, (dr, dc) in enumerate(AROUND):
            @pl.when(exists(dr, dc))
            def _(k=k):
                halo_copy(turn, k, source).start()

    def halo_wait(turn, source):
        for k, (dr, dc) in enumerate(AROUND):
            here = exists(-dr, -dc)

            @pl.when(here)
            def _(k=k):
                halo_copy(turn, k, source).wait_recv()

            @pl.when(jnp.logical_not(here))
            def _(dr=dr, dc=dc):
                if dc == 0:
                    rows_in[turn, 1 if dr < 0 else 0] = jnp.zeros((inner, width), BF16)
                else:
                    cols_in[turn, 1 if dc < 0 else 0, 1 - dr] = jnp.zeros((inner, width), F32)

        for k, (dr, dc) in enumerate(AROUND):
            @pl.when(exists(dr, dc))
            def _(k=k):
                halo_copy(turn, k, source).wait_send()

    def note_edges(turn, h, value):
        here = lane == h
        edge[turn, 0] = jnp.where(here, pltpu.roll(value, h, 1), edge[turn, 0])
        edge[turn, 1] = jnp.where(here, pltpu.roll(value, h + 1, 1), edge[turn, 1])

    def spread(turn, target):
        target[0, pl.ds(inner, inner)] = rows_in[turn, 0]
        target[height + 1, pl.ds(inner, inner)] = rows_in[turn, 1]
        sides = []
        for side in range(2):
            mid = pltpu.roll(cols_in[turn, side, 1], 1, 1)
            top_row = pltpu.roll(cols_in[turn, side, 0], width - height + 1, 1)
            low_row = pltpu.roll(cols_in[turn, side, 2], height + 1, 1)
            edge[turn, side] = jnp.where(lane == 0, top_row, jnp.where(lane == height + 1, low_row, mid))

        def one(p, _):
            value = target[p, pl.ds(inner, inner)].astype(F32)
            left = jnp.where(lane == 0, pltpu.roll(edge[turn, 0], lax.rem(width - p, width), 1),
                             pltpu.roll(value, 1, 1))
            right = jnp.where(lane == width - 1, pltpu.roll(edge[turn, 1], width - 1 - p, 1),
                              pltpu.roll(value, width - 1, 1))
            target[p, pl.ds(0, inner)] = left.astype(BF16)
            target[p, pl.ds(2 * inner, inner)] = right.astype(BF16)
            return 0

        lax.fori_loop(0, height + 2, one, 0)

    def joined(pieces):
        return jnp.concatenate(pieces, axis=1)

    def patch(source, h):
        return joined([source[pl.ds(h + r, 3)].reshape(9 * inner, width) for r in range(R)])

    def part(value, r):
        return value[:, r * width:(r + 1) * width]

    edge[...] = jnp.zeros_like(edge)
    tiles = 8

    def widen(src, dst):
        def one(i, _):
            block = src[pl.ds(i * tiles, tiles)].astype(F32)
            dst[pl.ds(pl.multiple_of(i * tiles * height, tiles * height), tiles * height)] = block.reshape(tiles * height, width)
            return 0

        lax.fori_loop(0, channels // tiles, one, 0)

    copy_x.wait()
    widen(xin, xf)

    def first(i, _):
        h = i * R
        pieces = []
        for r in range(R):
            piece = xf[pl.ds(h + r, channels, stride=height), :].astype(BF16)
            xb[h + r] = piece
            pieces.append(piece)
        value, grad = gelu_slope(dot(wrt[...], joined(pieces)))
        value = value.astype(BF16)
        for r in range(R):
            s1[h + r] = part(grad, r)
            hid[h + r + 1, pl.ds(inner, inner)] = part(value, r)
            note_edges(0, h + r, part(value, r).astype(F32))
        return 0

    lax.fori_loop(0, height // R, first, 0)
    halo_start(0, hid)
    copy_c.wait()
    widen(cin, cf)
    g_expand[...] = jnp.zeros_like(g_expand)
    g_spatial[...] = jnp.zeros_like(g_spatial)
    g_reduce[...] = jnp.zeros_like(g_reduce)
    halo_wait(0, hid)
    spread(0, hid)

    def second(i, _):
        h = i * R
        value, grad = gelu_slope(dot(w2[...], patch(hid, h)))
        value = value.astype(BF16)
        total = dot(wet[...], value) + joined([xb[h + r] for r in range(R)]).astype(F32)
        given = joined([cf[pl.ds(h + r, channels, stride=height), :] for r in range(R)])
        top = (given * slope(total)).astype(BF16)
        for r in range(R):
            tb[h + r] = part(top, r)
        g_expand[...] += dot_nt(value, top)
        behind = (dot(we[...], top) * grad).astype(BF16)
        for r in range(R):
            back[h + r + 1, pl.ds(inner, inner)] = part(behind, r)
            note_edges(1, h + r, part(behind, r).astype(F32))
        return 0

    lax.fori_loop(0, height // R, second, 0)
    halo_start(1, back)

    def third(i, _):
        h = i * R
        mine = joined([back[h + r + 1, pl.ds(inner, inner)] for r in range(R)])
        g_spatial[...] += dot_nt(patch(hid, h), mine)
        return 0

    lax.fori_loop(0, height // R, third, 0)
    halo_wait(1, back)
    spread(1, back)

    def fourth(i, _):
        h = i * R
        pre = dot(w3[...], patch(back, h))
        grad = joined([s1[h + r] for r in range(R)])
        one = (pre * grad).astype(BF16)
        g_reduce[...] += dot_nt(joined([xb[h + r] for r in range(R)]), one)
        result = dot(wr[...], one) + joined([tb[h + r] for r in range(R)]).astype(F32)
        for r in range(R):
            xf[pl.ds(h + r, channels, stride=height), :] = part(result, r)
        return 0

    lax.fori_loop(0, height // R, fourth, 0)

    def narrow(i, _):
        block = xf[pl.ds(pl.multiple_of(i * tiles * height, tiles * height), tiles * height)]
        out[pl.ds(i * tiles, tiles)] = block.reshape(tiles, height, width).astype(BF16)
        return 0

    lax.fori_loop(0, channels // tiles, narrow, 0)


def body(sizes, image, cotangent, w_reduce, w_spatial, w_expand):
    _, channels, height, width = image.shape
    inner = w_reduce.shape[1]
    count = lax.axis_size("dp") * lax.axis_size("row") * lax.axis_size("col")
    scale = float(height * width * count) ** (-0.5)
    w2 = w_spatial.reshape(9 * inner, inner).T
    w3 = jnp.transpose(w_spatial[::-1, ::-1], (2, 0, 1, 3)).reshape(inner, 9 * inner)
    vmem = pl.BlockSpec(memory_space=pltpu.VMEM)
    hbm = pl.BlockSpec(memory_space=pl.ANY)
    result, g_reduce, g_spatial, g_expand = pl.pallas_call(
        functools.partial(kernel, sizes),
        out_shape=(
            jax.ShapeDtypeStruct((channels, height, width), BF16),
            jax.ShapeDtypeStruct((channels, inner), F32),
            jax.ShapeDtypeStruct((9 * inner, inner), F32),
            jax.ShapeDtypeStruct((inner, channels), F32),
        ),
        in_specs=[hbm, hbm] + [vmem] * 6,
        out_specs=(vmem,) * 4,
        scratch_shapes=[
            pltpu.VMEM((channels, height, width), BF16),
            pltpu.VMEM((channels, height, width), BF16),
            pltpu.VMEM((channels * height, width), F32),
            pltpu.VMEM((channels * height, width), F32),
            pltpu.VMEM((height, channels, width), BF16),
            pltpu.VMEM((height, channels, width), BF16),
            pltpu.VMEM((height, inner, width), F32),
            pltpu.VMEM((height + 2, 3 * inner, width), BF16),
            pltpu.VMEM((height + 2, 3 * inner, width), BF16),
            pltpu.VMEM((2, 2, inner, width), F32),
            pltpu.VMEM((2, 2, inner, width), BF16),
            pltpu.VMEM((2, 2, 3, inner, width), F32),
            pltpu.SemaphoreType.DMA((2,)),
            pltpu.SemaphoreType.DMA((2, len(AROUND))),
            pltpu.SemaphoreType.DMA((2, len(AROUND))),
        ],
        compiler_params=pltpu.CompilerParams(
            collective_id=0, has_side_effects=True, vmem_limit_bytes=48 * 1024 * 1024),
    )(image[0], cotangent[0], w_reduce, w_reduce.T, w2, w3, w_expand, w_expand.T)
    g_reduce, g_spatial, g_expand = lax.psum(
        (g_reduce * scale, g_spatial.reshape(3, 3, inner, inner) * scale, g_expand * scale),
        ("dp", "row", "col"))
    return result[None], g_reduce, g_spatial, g_expand


def solution(mesh):
    sizes = (mesh.shape["row"], mesh.shape["col"])
    in_specs = (P("dp", None, "row", "col"), P("dp", None, "row", "col"), P(), P(), P())
    out_specs = (P("dp", None, "row", "col"), P(), P(), P())
    return jax.shard_map(functools.partial(body, sizes), mesh=mesh, in_specs=in_specs,
                         out_specs=out_specs, check_vma=False)
```

```python
import functools

import jax
import jax.numpy as jnp
from jax import lax
from jax.experimental import pallas as pl
from jax.experimental.pallas import tpu as pltpu
from jax.sharding import PartitionSpec as P

GELU_C = 0.7978845608028654
GELU_K = 0.044715
F32 = jnp.float32
BF16 = jnp.bfloat16
AROUND = ((-1, 0), (1, 0), (-1, -1), (0, -1), (1, -1), (-1, 1), (0, 1), (1, 1))
R = 2


def gelu_slope(v):
    v2 = v * v
    t = jnp.tanh(GELU_C * (v + GELU_K * v2 * v))
    half = 0.5 * (1.0 + t)
    return v * half, half + 0.5 * v * (1.0 - t * t) * (GELU_C * (1.0 + 3.0 * GELU_K * v2))


def slope(v):
    return gelu_slope(v)[1]


def dot(a, b):
    return lax.dot_general(a, b, (((1,), (0,)), ((), ())), preferred_element_type=F32)


def dot_nt(a, b):
    return lax.dot_general(a, b, (((1,), (1,)), ((), ())), preferred_element_type=F32)


def levels_of(sizes, rows):
    found = []
    for axis in ("col", "dp", "row"):
        count = sizes[axis]
        rows = -(-rows // (8 * count)) * 8
        found.append((axis, count, rows))
    return found


def kernel(sizes, scale, image, cot, wr, wrt, w2, w3, we, wet, out, o_reduce, o_spatial, o_expand,
           xin, cin, xf, cf, xb, tb, s1, hid, back, edge, rows_in, cols_in,
           g_reduce, g_spatial, g_expand, in_sem, send_sem, recv_sem, *sums):
    nrow, ncol = sizes["row"], sizes["col"]
    channels, height, width = image.shape
    inner = we.shape[0]
    row, col = lax.axis_index("row"), lax.axis_index("col")
    lane = lax.broadcasted_iota(jnp.int32, (inner, width), 1)

    copy_x = pltpu.make_async_copy(image, xin, in_sem.at[0])
    copy_c = pltpu.make_async_copy(cot, cin, in_sem.at[1])
    copy_x.start()
    copy_c.start()

    def exists(dr, dc):
        ok = jnp.bool_(True)
        if dr:
            ok = jnp.logical_and(ok, (row > 0) if dr < 0 else (row < nrow - 1))
        if dc:
            ok = jnp.logical_and(ok, (col > 0) if dc < 0 else (col < ncol - 1))
        return ok

    def peer_of(axis, count, step):
        return lax.rem(lax.axis_index(axis) + step, count)

    barrier = pltpu.get_barrier_semaphore()
    greeted = 0
    for axis, count in sizes.items():
        for step in range(1, count):
            pl.semaphore_signal(barrier, inc=1, device_id={axis: peer_of(axis, count, step)},
                                device_id_type=pl.DeviceIdType.MESH)
            greeted += 1
    for dr, dc in AROUND:
        if dr and dc:
            @pl.when(exists(dr, dc))
            def _(dr=dr, dc=dc):
                pl.semaphore_signal(barrier, inc=1, device_id={"row": row + dr, "col": col + dc},
                                    device_id_type=pl.DeviceIdType.MESH)
            greeted = greeted + exists(dr, dc).astype(jnp.int32)
    pl.semaphore_wait(barrier, greeted)

    def halo_copy(turn, k, source):
        dr, dc = AROUND[k]
        if dc == 0:
            src = source.at[1 if dr < 0 else height, pl.ds(inner, inner)]
            dst = rows_in.at[turn, 1 if dr < 0 else 0]
        else:
            src = edge.at[turn, 0 if dc < 0 else 1]
            dst = cols_in.at[turn, 1 if dc < 0 else 0, 1 - dr]
        return pltpu.make_async_remote_copy(
            src_ref=src, dst_ref=dst, send_sem=send_sem.at[turn, k], recv_sem=recv_sem.at[turn, k],
            device_id={"row": row + dr, "col": col + dc}, device_id_type=pl.DeviceIdType.MESH)

    def halo_start(turn, source):
        for k, (dr, dc) in enumerate(AROUND):
            @pl.when(exists(dr, dc))
            def _(k=k):
                halo_copy(turn, k, source).start()

    def halo_wait(turn, source):
        for k, (dr, dc) in enumerate(AROUND):
            here = exists(-dr, -dc)

            @pl.when(here)
            def _(k=k):
                halo_copy(turn, k, source).wait_recv()

            @pl.when(jnp.logical_not(here))
            def _(dr=dr, dc=dc):
                if dc == 0:
                    rows_in[turn, 1 if dr < 0 else 0] = jnp.zeros((inner, width), BF16)
                else:
                    cols_in[turn, 1 if dc < 0 else 0, 1 - dr] = jnp.zeros((inner, width), F32)

        for k, (dr, dc) in enumerate(AROUND):
            @pl.when(exists(dr, dc))
            def _(k=k):
                halo_copy(turn, k, source).wait_send()

    def note_edges(turn, h, value):
        here = lane == h
        edge[turn, 0] = jnp.where(here, pltpu.roll(value, h, 1), edge[turn, 0])
        edge[turn, 1] = jnp.where(here, pltpu.roll(value, h + 1, 1), edge[turn, 1])

    def spread(turn, target):
        target[0, pl.ds(inner, inner)] = rows_in[turn, 0]
        target[height + 1, pl.ds(inner, inner)] = rows_in[turn, 1]
        sides = []
        for side in range(2):
            mid = pltpu.roll(cols_in[turn, side, 1], 1, 1)
            top_row = pltpu.roll(cols_in[turn, side, 0], width - height + 1, 1)
            low_row = pltpu.roll(cols_in[turn, side, 2], height + 1, 1)
            edge[turn, side] = jnp.where(lane == 0, top_row, jnp.where(lane == height + 1, low_row, mid))

        def one(p, _):
            value = target[p, pl.ds(inner, inner)].astype(F32)
            left = jnp.where(lane == 0, pltpu.roll(edge[turn, 0], lax.rem(width - p, width), 1),
                             pltpu.roll(value, 1, 1))
            right = jnp.where(lane == width - 1, pltpu.roll(edge[turn, 1], width - 1 - p, 1),
                              pltpu.roll(value, width - 1, 1))
            target[p, pl.ds(0, inner)] = left.astype(BF16)
            target[p, pl.ds(2 * inner, inner)] = right.astype(BF16)
            return 0

        lax.fori_loop(0, height + 2, one, 0)

    def joined(pieces):
        return jnp.concatenate(pieces, axis=1)

    def patch(source, h):
        return joined([source[pl.ds(h + r, 3)].reshape(9 * inner, width) for r in range(R)])

    def part(value, r):
        return value[:, r * width:(r + 1) * width]

    edge[...] = jnp.zeros_like(edge)
    tiles = 8

    def widen(src, dst):
        def one(i, _):
            block = src[pl.ds(i * tiles, tiles)].astype(F32)
            dst[pl.ds(pl.multiple_of(i * tiles * height, tiles * height), tiles * height)] = block.reshape(tiles * height, width)
            return 0

        lax.fori_loop(0, channels // tiles, one, 0)

    copy_x.wait()
    widen(xin, xf)

    def first(i, _):
        h = i * R
        pieces = []
        for r in range(R):
            piece = xf[pl.ds(h + r, channels, stride=height), :].astype(BF16)
            xb[h + r] = piece
            pieces.append(piece)
        value, grad = gelu_slope(dot(wrt[...], joined(pieces)))
        value = value.astype(BF16)
        for r in range(R):
            s1[h + r] = part(grad, r)
            hid[h + r + 1, pl.ds(inner, inner)] = part(value, r)
            note_edges(0, h + r, part(value, r).astype(F32))
        return 0

    lax.fori_loop(0, height // R, first, 0)
    halo_start(0, hid)
    copy_c.wait()
    widen(cin, cf)
    g_expand[...] = jnp.zeros_like(g_expand)
    g_spatial[...] = jnp.zeros_like(g_spatial)
    g_reduce[...] = jnp.zeros_like(g_reduce)
    halo_wait(0, hid)
    spread(0, hid)

    def second(i, _):
        h = i * R
        value, grad = gelu_slope(dot(w2[...], patch(hid, h)))
        value = value.astype(BF16)
        total = dot(wet[...], value) + joined([xb[h + r] for r in range(R)]).astype(F32)
        given = joined([cf[pl.ds(h + r, channels, stride=height), :] for r in range(R)])
        top = (given * slope(total)).astype(BF16)
        for r in range(R):
            tb[h + r] = part(top, r)
        g_expand[...] += dot_nt(value, top)
        behind = (dot(we[...], top) * grad).astype(BF16)
        for r in range(R):
            back[h + r + 1, pl.ds(inner, inner)] = part(behind, r)
            note_edges(1, h + r, part(behind, r).astype(F32))
        return 0

    lax.fori_loop(0, height // R, second, 0)
    halo_start(1, back)

    def third(i, _):
        h = i * R
        mine = joined([back[h + r + 1, pl.ds(inner, inner)] for r in range(R)])
        g_spatial[...] += dot_nt(patch(hid, h), mine)
        return 0

    lax.fori_loop(0, height // R, third, 0)
    halo_wait(1, back)
    spread(1, back)

    def fourth(i, _):
        h = i * R
        pre = dot(w3[...], patch(back, h))
        grad = joined([s1[h + r] for r in range(R)])
        one = (pre * grad).astype(BF16)
        g_reduce[...] += dot_nt(one, joined([xb[h + r] for r in range(R)]))
        result = dot(wr[...], one) + joined([tb[h + r] for r in range(R)]).astype(F32)
        for r in range(R):
            xf[pl.ds(h + r, channels, stride=height), :] = part(result, r)
        return 0

    lax.fori_loop(0, height // R, fourth, 0)

    taps = g_spatial.shape[0] // 2
    wide = channels // 128
    total_rows = taps + 2 * wide * inner
    levels = levels_of(sizes, total_rows)
    near, far, landed = sums[0:3], sums[3:6], sums[6:9]
    sems = sums[9:]

    near[0][pl.ds(0, taps)] = joined([g_spatial[pl.ds(0, taps)], g_spatial[pl.ds(taps, taps)]])
    for k in range(wide):
        near[0][pl.ds(taps + k * inner, inner)] = g_expand[:, k * 128:(k + 1) * 128]
        near[0][pl.ds(taps + (wide + k) * inner, inner)] = g_reduce[:, k * 128:(k + 1) * 128]
    filled = total_rows
    for level, (axis, count, chunk) in enumerate(levels):
        if count * chunk > filled:
            near[level][pl.ds(filled, count * chunk - filled)] = jnp.zeros((count * chunk - filled, 128), F32)
        filled = chunk

    def send(level, step, gather):
        axis, count, chunk = levels[level]
        peer = peer_of(axis, count, step)
        if gather:
            mine = pl.ds(pl.multiple_of(lax.axis_index(axis) * chunk, 8), chunk)
            src, dst = far[level].at[mine], far[level].at[mine]
        else:
            src = near[level].at[pl.ds(pl.multiple_of(peer * chunk, 8), chunk)]
            dst = landed[level].at[step - 1]
        pair = sems[2 * level + (6 if gather else 0):]
        return pltpu.make_async_remote_copy(
            src_ref=src, dst_ref=dst, send_sem=pair[0].at[step - 1], recv_sem=pair[1].at[step - 1],
            device_id={axis: peer}, device_id_type=pl.DeviceIdType.MESH)

    for level, (axis, count, chunk) in enumerate(levels):
        copies = [send(level, step, False) for step in range(1, count)]
        for copy in copies:
            copy.start()
        mine = pl.ds(pl.multiple_of(lax.axis_index(axis) * chunk, 8), chunk)
        value = near[level][mine]
        for step, copy in enumerate(copies):
            copy.wait_recv()
            value = value + landed[level][step]
        if level < 2:
            near[level + 1][pl.ds(0, chunk)] = value
        else:
            far[level][mine] = value
        for copy in copies:
            copy.wait_send()
    for level in (2, 1, 0):
        axis, count, chunk = levels[level]
        if level < 2:
            far[level][pl.ds(pl.multiple_of(lax.axis_index(axis) * chunk, 8), chunk)] = far[level + 1][pl.ds(0, chunk)]
        copies = [send(level, step, True) for step in range(1, count)]
        for copy in copies:
            copy.start()
        for step in range(1, count):
            copies[step - 1].wait_recv()
        for copy in copies:
            copy.wait_send()
    both = far[0][pl.ds(0, taps)] * scale
    o_spatial[pl.ds(0, taps)] = both[:, :inner]
    o_spatial[pl.ds(taps, taps)] = both[:, inner:]
    for k in range(wide):
        o_expand[:, k * 128:(k + 1) * 128] = far[0][pl.ds(taps + k * inner, inner)] * scale
        o_reduce[:, k * 128:(k + 1) * 128] = far[0][pl.ds(taps + (wide + k) * inner, inner)] * scale

    def narrow(i, _):
        block = xf[pl.ds(pl.multiple_of(i * tiles * height, tiles * height), tiles * height)]
        out[pl.ds(i * tiles, tiles)] = block.reshape(tiles, height, width).astype(BF16)
        return 0

    lax.fori_loop(0, channels // tiles, narrow, 0)


def body(sizes, image, cotangent, w_reduce, w_spatial, w_expand):
    _, channels, height, width = image.shape
    inner = w_reduce.shape[1]
    count = lax.axis_size("dp") * lax.axis_size("row") * lax.axis_size("col")
    scale = float(height * width * count) ** (-0.5)
    w2 = w_spatial.reshape(9 * inner, inner).T
    w3 = jnp.transpose(w_spatial[::-1, ::-1], (2, 0, 1, 3)).reshape(inner, 9 * inner)
    levels = levels_of(sizes, (9 * inner * inner + 2 * inner * channels) // 128)
    vmem = pl.BlockSpec(memory_space=pltpu.VMEM)
    hbm = pl.BlockSpec(memory_space=pl.ANY)
    result, g_reduce, g_spatial, g_expand = pl.pallas_call(
        functools.partial(kernel, sizes, scale),
        out_shape=(
            jax.ShapeDtypeStruct((channels, height, width), BF16),
            jax.ShapeDtypeStruct((inner, channels), F32),
            jax.ShapeDtypeStruct((9 * inner, inner), F32),
            jax.ShapeDtypeStruct((inner, channels), F32),
        ),
        in_specs=[hbm, hbm] + [vmem] * 6,
        out_specs=(vmem,) * 4,
        scratch_shapes=[
            pltpu.VMEM((channels, height, width), BF16),
            pltpu.VMEM((channels, height, width), BF16),
            pltpu.VMEM((channels * height, width), F32),
            pltpu.VMEM((channels * height, width), F32),
            pltpu.VMEM((height, channels, width), BF16),
            pltpu.VMEM((height, channels, width), BF16),
            pltpu.VMEM((height, inner, width), F32),
            pltpu.VMEM((height + 2, 3 * inner, width), BF16),
            pltpu.VMEM((height + 2, 3 * inner, width), BF16),
            pltpu.VMEM((2, 2, inner, width), F32),
            pltpu.VMEM((2, 2, inner, width), BF16),
            pltpu.VMEM((2, 2, 3, inner, width), F32),
            pltpu.VMEM((inner, channels), F32),
            pltpu.VMEM((9 * inner, inner), F32),
            pltpu.VMEM((inner, channels), F32),
            pltpu.SemaphoreType.DMA((2,)),
            pltpu.SemaphoreType.DMA((2, len(AROUND))),
            pltpu.SemaphoreType.DMA((2, len(AROUND))),
        ] + [pltpu.VMEM((count * chunk, 128), F32) for _, count, chunk in levels]
        + [pltpu.VMEM((count * chunk, 128), F32) for _, count, chunk in levels]
        + [pltpu.VMEM((max(count - 1, 1), chunk, 128), F32) for _, count, chunk in levels]
        + [pltpu.SemaphoreType.DMA((max(count - 1, 1),))
           for _ in range(2) for _, count, _ in levels for _ in range(2)],
        compiler_params=pltpu.CompilerParams(
            collective_id=0, has_side_effects=True, vmem_limit_bytes=48 * 1024 * 1024),
    )(image[0], cotangent[0], w_reduce, w_reduce.T, w2, w3, w_expand, w_expand.T)
    return result[None], g_reduce.T, g_spatial.reshape(3, 3, inner, inner), g_expand


def solution(mesh):
    sizes = {axis: mesh.shape[axis] for axis in ("dp", "row", "col")}
    in_specs = (P("dp", None, "row", "col"), P("dp", None, "row", "col"), P(), P(), P())
    out_specs = (P("dp", None, "row", "col"), P(), P(), P())
    return jax.shard_map(functools.partial(body, sizes), mesh=mesh, in_specs=in_specs,
                         out_specs=out_specs, check_vma=False)
```
